32 devices in a mesh: dp: 4 (over z), expert: 8 (over y, x, core).
Axes of the slice: x: 2, y: 2, z: 4, core: 2. Of those that a mesh axis runs over, the one named last changes fastest.
Arguments:
- inputs: bfloat16 [1024, 2048], P('expert', 'dp'), may hold values from -6 to 6
- out_grad: bfloat16 [1024, 2048], P('expert', 'dp'), may hold values from -6 to 6
- gate_probs: float32 [1024, 2], P('expert'), may hold values from 0.1 to 1
- expert_ids: int32 [1024, 2], P('expert'), may hold values from 0 to 7, all different within a row; in each aligned block of 128 rows (0 to 127, 128 to 255, ...) at most 48 rows name the same one
- gate_proj: bfloat16 [8, 2048, 2304], P('expert', None, 'dp'), may hold values from -0.125 to 0.125
- down_proj: bfloat16 [8, 2304, 2048], P('expert', 'dp'), may hold values from -0.125 to 0.125
Outputs:
- layer_out: bfloat16 [1024, 2048], P('expert', 'dp')
- in_grad: bfloat16 [1024, 2048], P('expert', 'dp')
- prob_grad: float32 [1024, 2], P('expert')
The draws below stay inside these ranges and needn't reach their ends.
Inputs may be any that keep to these rules, and one draw needn't show every extreme that they name: `expert_ids`: each token names two different experts. Within each home group of 128 tokens no expert is named by more than 48 tokens, and in every draw some group names some expert exactly 48 times.
All inputs are finite; a program needn't handle non-finite values.
Results may differ from the reference program's by a relative error of at most 0.012.
Values may be sent and summed in bfloat16 or wider, within the bound.
A program may use at most 64 MiB of HBM per device.

```python
import math
import jax
import jax.numpy as jnp
import numpy as np
from jax import lax

D = 2048
HID_DEV = 576
TOK_DEV = 128
FF = 2304
EXPERTS = 8
CAP = 48
TOKENS = 1024


def shard_levels(own_key, extent, pieces, smallest, top_value):
    gain, own = 1.0, jax.random.fold_in(own_key, 6)
    for dim, shards_of in pieces:
        heights = jnp.exp(jax.random.uniform(jax.random.fold_in(own, dim), (shards_of,), jnp.float32, smallest / len(pieces), top_value / len(pieces)))
        gain = gain * jnp.repeat(heights, extent[dim] // shards_of).reshape([-1 if axis == dim else 1 for axis in range(len(extent))])
    return gain


def assign_block(stream_key, own, number, rows, count, top, reach, lean):
    ranking = jax.random.permutation(stream_key, count)
    heavy_load, ordinary = portions_of(count, rows * top, reach, lean, True), portions_of(count, rows * top, reach, lean, False)
    places = jnp.arange(count)

    def named(tallies, rotation):
        used = int((tallies > 0).sum())
        fixed = max(1, used // 4)
        passed = fixed + (places - fixed + rotation * (used - fixed)) % max(1, count - fixed)
        return jnp.zeros((count,), jnp.int32).at[ranking[jnp.where(places < fixed, places, passed)]].set(jnp.asarray(tallies, jnp.int32))

    tallies = jnp.where(number % 4 == 0, named(heavy_load, number // 4), named(ordinary, number - number // 4 - 1))
    mixed = jax.random.permutation(jax.random.fold_in(own, 3), count)
    donor, receiver = mixed[0:count // 2 * 2:2], mixed[1:count // 2 * 2:2]
    room = jnp.minimum(tallies[donor] - 1, reach - tallies[receiver]) // 2
    room = jnp.where((donor == ranking[0]) | (receiver == ranking[0]) | (tallies[receiver] == 0), 0, jnp.maximum(room, 0))
    passed = jax.random.randint(jax.random.fold_in(own, 4), (count // 2,), 0, 1 << 20) % (room + 1)
    tallies = tallies.at[donor].add(-passed).at[receiver].add(passed)
    items = jnp.searchsorted(jnp.cumsum(tallies), jnp.arange(rows * top), side="right").astype(jnp.int32)
    table = items.reshape(top, rows).T
    table = table[jax.random.permutation(jax.random.fold_in(own, 1), rows)]
    rotation = jax.random.randint(jax.random.fold_in(own, 2), (rows, 1), 0, top)
    return jnp.take_along_axis(table, (jnp.arange(top)[None, :] + rotation) % top, axis=1)


def portions_of(amount, total, limit, slope, full):
    loads = [(1 << 20) // math.isqrt(grade ** slope) + 1 for grade in range(1, amount + 1)]
    largest = limit if full else min(limit, max(-(-total // amount), total * loads[0] // sum(loads)))
    least = 1 if total - largest >= amount - 1 else 0
    counts, surplus = [largest] + [least] * (amount - 1), total - largest - least * (amount - 1)
    while surplus > 0:
        candidates = [i for i in range(1, amount) if counts[i] < largest] or [i for i in range(1, amount) if counts[i] < limit]
        whole, left = sum([loads[i] for i in candidates]), surplus
        for i in candidates:
            addition = min(limit - counts[i], max(1, left * loads[i] // whole), surplus)
            counts[i] = counts[i] + addition
            surplus = surplus - addition
    return np.array(counts)


def gaussian(own_key, dims, deviation, reach, cuts=(), kind=jnp.bfloat16):
    values = deviation * jax.random.normal(own_key, dims, jnp.float32)
    if cuts:
        values = values * shard_levels(own_key, dims, cuts, -0.22, 0.18)
    return jnp.clip(values, -reach, reach).astype(kind)


def setup_inputs(seed: int = 0) -> dict:
    key_list = jax.random.split(jax.random.key(seed), 7)
    inputs = gaussian(key_list[0], (TOKENS, D), 1.0, 6.0, ((0, 8), (1, 4)))
    out_grad = gaussian(key_list[1], (TOKENS, D), 1.0, 6.0, ((0, 8), (1, 4)))
    gate_probs = jnp.clip(0.1 + 0.9 * jax.random.uniform(key_list[2], (TOKENS, 2), jnp.float32) ** shard_levels(key_list[2], (TOKENS, 2), ((0, 8),), -0.2, 0.2), 0.1, 1.0)
    expert_ids_keys = jax.random.split(jax.random.fold_in(key_list[3], 1), TOKENS // TOK_DEV)
    expert_ids_turns = jax.random.permutation(jax.random.fold_in(key_list[3], 3), TOKENS // TOK_DEV)
    expert_ids = jax.vmap(lambda own, number: assign_block(jax.random.fold_in(key_list[3], 2), own, number, TOK_DEV, EXPERTS, 2, CAP, 2))(expert_ids_keys, expert_ids_turns).reshape((TOKENS, 2))
    gate_proj = gaussian(key_list[4], (EXPERTS, D, FF), D ** -0.5, 0.125, ((0, 8), (2, 4)))
    down_proj = gaussian(key_list[5], (EXPERTS, FF, D), FF ** -0.5, 0.125, ((0, 8), (1, 4)))
    return {"inputs": inputs, "out_grad": out_grad, "gate_probs": gate_probs, "expert_ids": expert_ids, "gate_proj": gate_proj, "down_proj": down_proj}


def block_sum(parts):
    rounded = lax.optimization_barrier(parts.astype(jnp.bfloat16))
    return jnp.sum(rounded.astype(jnp.float32), axis=0).astype(jnp.bfloat16)


def reference(inputs, out_grad, gate_probs, expert_ids, gate_proj, down_proj):
    homes = EXPERTS
    blocks = FF // HID_DEV
    copies = 2 * TOK_DEV
    flat = expert_ids.reshape(homes, copies)
    onehot = (flat[:, :, None] == jnp.arange(EXPERTS, dtype=jnp.int32)[None, None, :]).astype(jnp.int32)
    before = jnp.cumsum(onehot, axis=1) - onehot
    position = jnp.sum(before * onehot, axis=2).astype(jnp.int32)
    home = jnp.broadcast_to(jnp.arange(homes, dtype=jnp.int32)[:, None], (homes, copies))
    copy_id = home * copies + jnp.arange(copies, dtype=jnp.int32)[None, :]
    table = jnp.full((EXPERTS, homes, CAP), 2 * TOKENS, jnp.int32).at[flat, home, position].set(copy_id)
    table = table.reshape(EXPERTS, homes * CAP)
    x_pad = jnp.concatenate([inputs, jnp.zeros((1, D), jnp.bfloat16)], axis=0)
    dy_pad = jnp.concatenate([out_grad, jnp.zeros((1, D), jnp.bfloat16)], axis=0)
    p_pad = jnp.concatenate([gate_probs.reshape(-1), jnp.zeros((1,), jnp.float32)])

    def one_expert(pack):
        w_gate, w_down, slots = pack
        token = jnp.where(slots < 2 * TOKENS, slots // 2, TOKENS).astype(jnp.int32)
        x_rows = x_pad[token]
        prob = p_pad[slots][:, None]
        pre_gate = jnp.dot(x_rows, w_gate, preferred_element_type=jnp.float32)
        sig = jax.nn.sigmoid(pre_gate)
        hidden = (pre_gate * sig).astype(jnp.bfloat16)
        rows = hidden.shape[0]
        out_parts = jnp.einsum('rnh,nhd->nrd', hidden.reshape(rows, blocks, HID_DEV).astype(jnp.float32),
                               w_down.reshape(blocks, HID_DEV, D).astype(jnp.float32))
        expert_out = block_sum(out_parts)
        slot_grad = (prob * dy_pad[token].astype(jnp.float32)).astype(jnp.bfloat16)
        back = lax.dot_general(slot_grad, w_down, (((1,), (1,)), ((), ())), preferred_element_type=jnp.float32)
        gate_term = (back * sig * (1.0 + pre_gate * (1.0 - sig))).astype(jnp.bfloat16)
        in_parts = jnp.einsum('rnh,dnh->nrd', gate_term.reshape(rows, blocks, HID_DEV).astype(jnp.float32),
                              w_gate.reshape(D, blocks, HID_DEV).astype(jnp.float32))
        copy_grad = block_sum(in_parts)
        return expert_out, copy_grad

    expert_out, copy_grad = lax.map(one_expert, (gate_proj, down_proj, table))
    where = home * CAP + position
    out_copy = expert_out[flat, where].reshape(TOKENS, 2, D).astype(jnp.float32)
    grad_copy = copy_grad[flat, where].reshape(TOKENS, 2, D).astype(jnp.float32)
    layer_out = jnp.sum(gate_probs[:, :, None] * out_copy, axis=1).astype(jnp.bfloat16)
    in_grad = jnp.sum(grad_copy, axis=1).astype(jnp.bfloat16)
    prob_grad = jnp.sum(out_grad.astype(jnp.float32)[:, None, :] * out_copy, axis=2)
    return layer_out, in_grad, prob_grad
```

```python
import functools

import jax
import jax.numpy as jnp
from jax import lax
from jax.experimental import pallas as pl
from jax.experimental.pallas import tpu as pltpu
from jax.sharding import PartitionSpec as P

MESH = pl.DeviceIdType.MESH
LANES = 128


def flip(a, b, size):
    out, bit = 0, 1
    while bit < size:
        out = out + ((a // bit + b // bit) % 2) * bit
        bit *= 2
    return out


def nt_dot(left, right):
    return lax.dot_general(
        left, right, (((1,), (1,)), ((), ())), preferred_element_type=jnp.float32
    )


def nn_dot(left, right):
    return jnp.dot(left, right, preferred_element_type=jnp.float32)


def moe_kernel(
    parts, experts, cap,
    x_ref, dy_ref, p_ref, id_ref, wg_hbm, wd_hbm,
    lo_ref, ig_ref, pg_ref,
    wg, wd, home, pick0, pick1, spread, weight,
    send, recv, pre, back, hid, gterm, rsend, rrecv,
    part, gathered, own, pacc, psend, precv,
    w_sem, ag_send, ag_recv, loc_sem, a_send, a_recv, rloc_sem, r_send, r_recv,
    s_send, s_recv, p_send, p_recv,
):
    z = lax.axis_index("dp")
    me = lax.axis_index("expert")
    tokens, cols = x_ref.shape
    rows = experts * cap
    bf16, f32 = jnp.bfloat16, jnp.float32

    load_g = pltpu.make_async_copy(wg_hbm.at[0], wg, w_sem.at[0])
    load_d = pltpu.make_async_copy(wd_hbm.at[0], wd, w_sem.at[1])
    load_g.start()
    load_d.start()

    barrier = pltpu.get_barrier_semaphore()

    @pl.loop(1, parts)
    def _(i):
        pl.semaphore_signal(
            barrier, inc=1, device_id={"dp": flip(z, i, parts)}, device_id_type=MESH
        )

    @pl.loop(1, experts)
    def _(j):
        pl.semaphore_signal(
            barrier, inc=1, device_id={"expert": flip(me, j, experts)}, device_id_type=MESH
        )

    ids = id_ref[...]
    probs = p_ref[...]
    id0, id1 = ids[:, 0:1], ids[:, 1:2]
    p0, p1 = probs[:, 0:1], probs[:, 1:2]
    lane = lax.broadcasted_iota(jnp.int32, (tokens, LANES), 1)
    hot0 = (lane == id0).astype(f32)
    hot1 = (lane == id1).astype(f32)
    earlier = (
        lax.broadcasted_iota(jnp.int32, (tokens, tokens), 1)
        < lax.broadcasted_iota(jnp.int32, (tokens, tokens), 0)
    ).astype(f32)
    count = nn_dot(earlier.astype(bf16), (hot0 + hot1).astype(bf16))
    pos0 = jnp.sum(count * hot0, axis=1, keepdims=True)
    pos1 = jnp.sum(count * hot1, axis=1, keepdims=True)
    slot = lax.broadcasted_iota(jnp.int32, (tokens, rows), 1)
    t0 = (slot == id0 * cap + pos0.astype(jnp.int32)).astype(f32)
    t1 = (slot == id1 * cap + pos1.astype(jnp.int32)).astype(f32)
    pick0[...] = t0.astype(bf16)
    pick1[...] = t1.astype(bf16)
    spread[...] = jnp.transpose(t0 + t1).astype(bf16)
    weight[...] = jnp.sum(jnp.transpose(t0 * p0 + t1 * p1), axis=1, keepdims=True)

    home[z, 0] = x_ref[...]
    home[z, 1] = dy_ref[...]
    pre[...] = jnp.zeros_like(pre)
    back[...] = jnp.zeros_like(back)
    pacc[...] = jnp.zeros_like(pacc)

    pl.semaphore_wait(barrier, parts - 1 + experts - 1)

    def to_home(i):
        peer = flip(z, i, parts)
        return pltpu.make_async_remote_copy(
            src_ref=home.at[z], dst_ref=home.at[z],
            send_sem=ag_send, recv_sem=ag_recv.at[z],
            device_id={"dp": peer}, device_id_type=MESH,
        )

    @pl.loop(1, parts)
    def _(i):
        to_home(i).start()

    def exchange(source, target, chunk, send_sem, recv_sem, local_sem):
        @pl.loop(1, experts)
        def _(j):
            peer = flip(me, experts - j, experts)
            pltpu.make_async_remote_copy(
                src_ref=source.at[chunk, peer], dst_ref=target.at[chunk, me],
                send_sem=send_sem, recv_sem=recv_sem.at[chunk],
                device_id={"expert": peer}, device_id_type=MESH,
            ).start()
        pltpu.make_async_copy(
            source.at[chunk, me], target.at[chunk, me], local_sem.at[chunk]
        ).start()

    def exchanged(source, target, chunk, send_sem, recv_sem, local_sem):
        pltpu.make_async_copy(
            source.at[chunk, me], target.at[chunk, me], local_sem.at[chunk]
        ).wait()
        several = target.at[chunk, pl.ds(0, experts - 1)]
        pltpu.make_async_copy(several, several, recv_sem.at[chunk]).wait()

    def dispatch(chunk):
        xs = nn_dot(spread[...], home[chunk, 0]).astype(bf16)
        gs = (weight[...] * nn_dot(spread[...], home[chunk, 1])).astype(bf16)
        send[chunk, :, 0:cap] = xs.reshape(experts, cap, cols)
        send[chunk, :, cap:] = gs.reshape(experts, cap, cols)
        exchange(send, recv, chunk, a_send, a_recv, loc_sem)

    dispatch(z)

    @pl.loop(1, parts)
    def _(i):
        chunk = flip(z, i, parts)
        pltpu.make_async_copy(home.at[chunk], home.at[chunk], ag_recv.at[chunk]).wait()
        dispatch(chunk)

    load_g.wait()
    load_d.wait()

    @pl.loop(0, parts)
    def _(i):
        chunk = flip(z, i, parts)
        start = pl.multiple_of(chunk * cols, cols)
        exchanged(send, recv, chunk, a_send, a_recv, loc_sem)
        xr = recv[chunk, :, 0:cap].reshape(rows, cols)
        gr = recv[chunk, :, cap:].reshape(rows, cols)
        pre[...] += nn_dot(xr, wg[pl.ds(start, cols), :])
        back[...] += nt_dot(gr, wd[:, pl.ds(start, cols)])

    v = pre[...]
    sig = jax.nn.sigmoid(v)
    hid[...] = (v * sig).astype(bf16)
    gterm[...] = (back[...] * sig * (1.0 + v * (1.0 - sig))).astype(bf16)

    @pl.loop(1, parts + 1)
    def _(i):
        chunk = flip(z, i % parts, parts)
        start = pl.multiple_of(chunk * cols, cols)
        out = nn_dot(hid[...], wd[:, pl.ds(start, cols)]).astype(bf16)
        grad = nt_dot(gterm[...], wg[pl.ds(start, cols), :]).astype(bf16)
        rsend[chunk, :, 0:cap] = out.reshape(experts, cap, cols)
        rsend[chunk, :, cap:] = grad.reshape(experts, cap, cols)
        exchange(rsend, rrecv, chunk, r_send, r_recv, rloc_sem)

    def combine(chunk):
        exchanged(rsend, rrecv, chunk, r_send, r_recv, rloc_sem)
        out = rrecv[chunk, :, 0:cap].reshape(rows, cols)
        grad = rrecv[chunk, :, cap:].reshape(rows, cols)
        out0, out1 = nn_dot(pick0[...], out), nn_dot(pick1[...], out)
        dy = home[chunk, 1].astype(f32)
        s0 = jnp.sum(dy * out0, axis=1, keepdims=True)
        s1 = jnp.sum(dy * out1, axis=1, keepdims=True)
        pacc[...] += jnp.where(lane == 0, s0, 0.0) + jnp.where(lane == 1, s1, 0.0)
        weights = p_ref[...]
        layer = weights[:, 0:1] * out0 + weights[:, 1:2] * out1
        return layer, nn_dot(pick0[...] + pick1[...], grad)

    def to_owner(chunk):
        return pltpu.make_async_remote_copy(
            src_ref=part.at[chunk], dst_ref=gathered.at[z],
            send_sem=s_send, recv_sem=s_recv,
            device_id={"dp": chunk}, device_id_type=MESH,
        )

    @pl.loop(1, parts)
    def _(i):
        chunk = flip(z, i, parts)
        layer, grad = combine(chunk)
        part[chunk, 0] = layer.astype(bf16)
        part[chunk, 1] = grad.astype(bf16)
        to_owner(chunk).start()

    layer, grad = combine(z)
    own[0] = layer
    own[1] = grad
    psend[...] = jnp.transpose(pacc[...])[0:8]

    @pl.loop(1, parts)
    def _(i):
        pltpu.make_async_remote_copy(
            src_ref=psend, dst_ref=precv.at[z],
            send_sem=p_send, recv_sem=p_recv,
            device_id={"dp": flip(z, i, parts)}, device_id_type=MESH,
        ).start()

    others = gathered.at[pl.ds(0, parts - 1)]
    pltpu.make_async_copy(others, others, s_recv).wait()

    @pl.loop(1, parts)
    def _(i):
        other = flip(z, i, parts)
        own[...] += gathered[other].astype(f32)

    lo_ref[...] = own[0].astype(bf16)
    ig_ref[...] = own[1].astype(bf16)

    rest = precv.at[pl.ds(0, parts - 1)]
    pltpu.make_async_copy(rest, rest, p_recv).wait()
    pg_ref[...] = psend[...]

    @pl.loop(1, parts)
    def _(i):
        pg_ref[...] += precv[flip(z, i, parts)]

    sent = home.at[pl.ds(0, parts - 1)]
    pltpu.make_async_copy(sent, sent, ag_send).wait()
    pltpu.make_async_copy(others, others, s_send).wait()
    pltpu.make_async_copy(rest, rest, p_send).wait()
    several = send.at[0, pl.ds(0, experts - 1)]

    @pl.loop(0, parts)
    def _(i):
        pltpu.make_async_copy(several, several, a_send).wait()
        pltpu.make_async_copy(several, several, r_send).wait()


def per_device(inputs, out_grad, gate_probs, expert_ids, gate_proj, down_proj):
    parts = lax.axis_size("dp")
    experts = lax.axis_size("expert")
    tokens, cols = inputs.shape
    cap = -(-(3 * tokens // experts) // 16) * 16
    rows = experts * cap
    _, width, hidden = gate_proj.shape
    bf16, f32 = jnp.bfloat16, jnp.float32
    vmem = pl.BlockSpec(memory_space=pltpu.VMEM)
    hbm = pl.BlockSpec(memory_space=pl.ANY)
    dma = pltpu.SemaphoreType.DMA
    layer_out, in_grad, prob = pl.pallas_call(
        functools.partial(moe_kernel, parts, experts, cap),
        out_shape=(
            jax.ShapeDtypeStruct((tokens, cols), bf16),
            jax.ShapeDtypeStruct((tokens, cols), bf16),
            jax.ShapeDtypeStruct((8, tokens), f32),
        ),
        in_specs=[vmem, vmem, vmem, vmem, hbm, hbm],
        out_specs=(vmem, vmem, vmem),
        scratch_shapes=[
            pltpu.VMEM((width, hidden), bf16),
            pltpu.VMEM((hidden, width), bf16),
            pltpu.VMEM((parts, 2, tokens, cols), bf16),
            pltpu.VMEM((tokens, rows), bf16),
            pltpu.VMEM((tokens, rows), bf16),
            pltpu.VMEM((rows, tokens), bf16),
            pltpu.VMEM((rows, 1), f32),
            pltpu.VMEM((parts, experts, 2 * cap, cols), bf16),
            pltpu.VMEM((parts, experts, 2 * cap, cols), bf16),
            pltpu.VMEM((rows, hidden), f32),
            pltpu.VMEM((rows, hidden), f32),
            pltpu.VMEM((rows, hidden), bf16),
            pltpu.VMEM((rows, hidden), bf16),
            pltpu.VMEM((parts, experts, 2 * cap, cols), bf16),
            pltpu.VMEM((parts, experts, 2 * cap, cols), bf16),
            pltpu.VMEM((parts, 2, tokens, cols), bf16),
            pltpu.VMEM((parts, 2, tokens, cols), bf16),
            pltpu.VMEM((2, tokens, cols), f32),
            pltpu.VMEM((tokens, LANES), f32),
            pltpu.VMEM((8, tokens), f32),
            pltpu.VMEM((parts, 8, tokens), f32),
            dma((2,)), dma, dma((parts,)), dma((parts,)), dma, dma((parts,)),
            dma((parts,)), dma, dma((parts,)), dma, dma, dma, dma,
        ],
        compiler_params=pltpu.CompilerParams(
            collective_id=0, has_side_effects=True, vmem_limit_bytes=56 * 1024 * 1024
        ),
    )(inputs, out_grad, gate_probs, expert_ids, gate_proj, down_proj)
    return layer_out, in_grad, prob[:2].T


def solution(mesh):
    placed = (
        P("expert", "dp"),
        P("expert", "dp"),
        P("expert", None),
        P("expert", None),
        P("expert", None, "dp"),
        P("expert", "dp", None),
    )
    return jax.shard_map(
        per_device,
        mesh=mesh,
        in_specs=placed,
        out_specs=(P("expert", "dp"), P("expert", "dp"), P("expert", None)),
        check_vma=False,
    )
```

```python
import functools

import jax
import jax.numpy as jnp
from jax import lax
from jax.experimental import pallas as pl
from jax.experimental.pallas import tpu as pltpu
from jax.sharding import PartitionSpec as P

MESH = pl.DeviceIdType.MESH
LANES = 128


def flip(a, b, size):
    out, bit = 0, 1
    while bit < size:
        out = out + ((a // bit + b // bit) % 2) * bit
        bit *= 2
    return out


def nt_dot(left, right):
    return lax.dot_general(
        left, right, (((1,), (1,)), ((), ())), preferred_element_type=jnp.float32
    )


def nn_dot(left, right):
    return jnp.dot(left, right, preferred_element_type=jnp.float32)


def moe_kernel(
    parts, experts, cap,
    x_ref, dy_ref, p_ref, id_ref, wg_hbm, wd_hbm,
    both_ref, pg_ref,
    wg, wd, home, pick0, pick1, spread, weight,
    send, recv, pre, back, hid, gterm, rsend, rrecv,
    part, gathered, own, pacc, psend, precv,
    w_sem, ag_send, ag_recv, loc_sem, a_send, a_recv, rloc_sem, r_send, r_recv,
    s_send, s_recv, p_send, p_recv,
):
    z = lax.axis_index("dp")
    me = lax.axis_index("expert")
    tokens, cols = x_ref.shape
    rows = experts * cap
    bf16, f32 = jnp.bfloat16, jnp.float32

    load_g = pltpu.make_async_copy(wg_hbm.at[0], wg, w_sem.at[0])
    load_d = pltpu.make_async_copy(wd_hbm.at[0], wd, w_sem.at[1])
    load_g.start()
    load_d.start()

    barrier = pltpu.get_barrier_semaphore()

    @pl.loop(1, parts)
    def _(i):
        pl.semaphore_signal(
            barrier, inc=1, device_id={"dp": flip(z, i, parts)}, device_id_type=MESH
        )

    @pl.loop(1, experts)
    def _(j):
        pl.semaphore_signal(
            barrier, inc=1, device_id={"expert": flip(me, j, experts)}, device_id_type=MESH
        )

    across = lax.broadcasted_iota(jnp.int32, (tokens, tokens), 1)
    down = lax.broadcasted_iota(jnp.int32, (tokens, tokens), 0)

    def column(row):
        return jnp.sum(jnp.where(across == down, row, 0), axis=1, keepdims=True)

    id0, id1 = column(id_ref[0:1, :]), column(id_ref[1:2, :])
    p0, p1 = column(p_ref[0:1, :]), column(p_ref[1:2, :])
    lane = lax.broadcasted_iota(jnp.int32, (tokens, LANES), 1)
    hot0 = (lane == id0).astype(f32)
    hot1 = (lane == id1).astype(f32)
    earlier = (across < down).astype(f32)
    count = nn_dot(earlier.astype(bf16), (hot0 + hot1).astype(bf16))
    pos0 = jnp.sum(count * hot0, axis=1, keepdims=True)
    pos1 = jnp.sum(count * hot1, axis=1, keepdims=True)
    slot = lax.broadcasted_iota(jnp.int32, (tokens, rows), 1)
    t0 = (slot == id0 * cap + pos0.astype(jnp.int32)).astype(f32)
    t1 = (slot == id1 * cap + pos1.astype(jnp.int32)).astype(f32)
    pick0[...] = t0.astype(bf16)
    pick1[...] = t1.astype(bf16)
    spread[...] = jnp.transpose(t0 + t1).astype(bf16)
    weight[...] = jnp.sum(jnp.transpose(t0 * p0 + t1 * p1), axis=1, keepdims=True)

    home[z, 0] = x_ref[...]
    home[z, 1] = dy_ref[...]
    pre[...] = jnp.zeros_like(pre)
    back[...] = jnp.zeros_like(back)
    pacc[...] = jnp.zeros_like(pacc)

    with jax.named_scope("entry"):
        pl.semaphore_wait(barrier, parts - 1 + experts - 1)

    def to_home(i):
        peer = flip(z, i, parts)
        return pltpu.make_async_remote_copy(
            src_ref=home.at[z], dst_ref=home.at[z],
            send_sem=ag_send, recv_sem=ag_recv.at[z],
            device_id={"dp": peer}, device_id_type=MESH,
        )

    @pl.loop(1, parts)
    def _(i):
        to_home(i).start()

    def exchange(source, target, chunk, send_sem, recv_sem, local_sem):
        @pl.loop(1, experts)
        def _(j):
            peer = flip(me, experts - j, experts)
            pltpu.make_async_remote_copy(
                src_ref=source.at[chunk, peer], dst_ref=target.at[chunk, me],
                send_sem=send_sem, recv_sem=recv_sem.at[chunk],
                device_id={"expert": peer}, device_id_type=MESH,
            ).start()
        pltpu.make_async_copy(
            source.at[chunk, me], target.at[chunk, me], local_sem.at[chunk]
        ).start()

    def exchanged(source, target, chunk, send_sem, recv_sem, local_sem):
        pltpu.make_async_copy(
            source.at[chunk, me], target.at[chunk, me], local_sem.at[chunk]
        ).wait()
        several = target.at[chunk, pl.ds(0, experts - 1)]
        pltpu.make_async_copy(several, several, recv_sem.at[chunk]).wait()

    def dispatch(chunk):
        xs = nn_dot(spread[...], home[chunk, 0]).astype(bf16)
        gs = (weight[...] * nn_dot(spread[...], home[chunk, 1])).astype(bf16)
        send[chunk, :, 0:cap] = xs.reshape(experts, cap, cols)
        send[chunk, :, cap:] = gs.reshape(experts, cap, cols)
        exchange(send, recv, chunk, a_send, a_recv, loc_sem)

    with jax.named_scope("dispatch_own"):
        dispatch(z)

    @pl.loop(1, parts)
    def _(i):
        chunk = flip(z, i, parts)
        with jax.named_scope("home_wait"):
            pltpu.make_async_copy(home.at[chunk], home.at[chunk], ag_recv.at[chunk]).wait()
        with jax.named_scope("dispatch"):
            dispatch(chunk)

    load_g.wait()
    load_d.wait()

    @pl.loop(0, parts)
    def _(i):
        chunk = flip(z, i, parts)
        start = pl.multiple_of(chunk * cols, cols)
        with jax.named_scope("rows_wait"):
            exchanged(send, recv, chunk, a_send, a_recv, loc_sem)
        xr = recv[chunk, :, 0:cap].reshape(rows, cols)
        gr = recv[chunk, :, cap:].reshape(rows, cols)
        pre[...] += nt_dot(xr, wg[:, pl.ds(start, cols)])
        back[...] += nt_dot(gr, wd[:, pl.ds(start, cols)])

    with jax.named_scope("activation"):
        v = pre[...]
        sig = jax.nn.sigmoid(v)
        hid[...] = (v * sig).astype(bf16)
        gterm[...] = (back[...] * sig * (1.0 + v * (1.0 - sig))).astype(bf16)

    @pl.loop(1, parts + 1)
    def _(i):
        chunk = flip(z, i % parts, parts)
        start = pl.multiple_of(chunk * cols, cols)
        out = nn_dot(hid[...], wd[:, pl.ds(start, cols)]).astype(bf16)
        grad = nn_dot(gterm[...], wg[:, pl.ds(start, cols)]).astype(bf16)
        rsend[chunk, :, 0:cap] = out.reshape(experts, cap, cols)
        rsend[chunk, :, cap:] = grad.reshape(experts, cap, cols)
        exchange(rsend, rrecv, chunk, r_send, r_recv, rloc_sem)

    def combine(chunk):
        with jax.named_scope("back_wait"):
            exchanged(rsend, rrecv, chunk, r_send, r_recv, rloc_sem)
        out = rrecv[chunk, :, 0:cap].reshape(rows, cols)
        grad = rrecv[chunk, :, cap:].reshape(rows, cols)
        out0, out1 = nn_dot(pick0[...], out), nn_dot(pick1[...], out)
        dy = home[chunk, 1].astype(f32)
        s0 = jnp.sum(dy * out0, axis=1, keepdims=True)
        s1 = jnp.sum(dy * out1, axis=1, keepdims=True)
        pacc[...] += jnp.where(lane == 0, s0, 0.0) + jnp.where(lane == 1, s1, 0.0)
        layer = p0 * out0 + p1 * out1
        return layer, nn_dot(pick0[...] + pick1[...], grad)

    def to_owner(chunk):
        return pltpu.make_async_remote_copy(
            src_ref=part.at[chunk], dst_ref=gathered.at[z],
            send_sem=s_send, recv_sem=s_recv,
            device_id={"dp": chunk}, device_id_type=MESH,
        )

    @pl.loop(1, parts)
    def _(i):
        chunk = flip(z, i, parts)
        layer, grad = combine(chunk)
        part[chunk, 0] = layer.astype(bf16)
        part[chunk, 1] = grad.astype(bf16)
        to_owner(chunk).start()

    layer, grad = combine(z)
    own[0] = layer
    own[1] = grad
    psend[...] = jnp.transpose(pacc[...])[0:8]

    @pl.loop(1, parts)
    def _(i):
        pltpu.make_async_remote_copy(
            src_ref=psend, dst_ref=precv.at[z],
            send_sem=p_send, recv_sem=p_recv,
            device_id={"dp": flip(z, i, parts)}, device_id_type=MESH,
        ).start()

    others = gathered.at[pl.ds(0, parts - 1)]
    with jax.named_scope("sums_wait"):
        pltpu.make_async_copy(others, others, s_recv).wait()

    @pl.loop(1, parts)
    def _(i):
        other = flip(z, i, parts)
        own[...] += gathered[other].astype(f32)

    both_ref[...] = own[...].astype(bf16)

    rest = precv.at[pl.ds(0, parts - 1)]
    with jax.named_scope("prob_wait"):
        pltpu.make_async_copy(rest, rest, p_recv).wait()
    pg_ref[...] = psend[0:2]

    @pl.loop(1, parts)
    def _(i):
        pg_ref[...] += precv[flip(z, i, parts), 0:2]

    sent = home.at[pl.ds(0, parts - 1)]
    pltpu.make_async_copy(sent, sent, ag_send).wait()
    pltpu.make_async_copy(others, others, s_send).wait()
    pltpu.make_async_copy(rest, rest, p_send).wait()
    several = send.at[0, pl.ds(0, experts - 1)]

    @pl.loop(0, parts)
    def _(i):
        pltpu.make_async_copy(several, several, a_send).wait()
        pltpu.make_async_copy(several, several, r_send).wait()


def split_kernel(both_ref, prob_ref, lo_ref, ig_ref, pg_ref):
    lo_ref[...] = both_ref[0]
    ig_ref[...] = both_ref[1]
    pg_ref[...] = prob_ref[...]


def per_device(inputs, out_grad, gate_probs, expert_ids, gate_proj, down_proj):
    parts = lax.axis_size("dp")
    experts = lax.axis_size("expert")
    tokens, cols = inputs.shape
    cap = -(-(3 * tokens // experts) // 16) * 16
    rows = experts * cap
    _, width, hidden = gate_proj.shape
    bf16, f32 = jnp.bfloat16, jnp.float32
    vmem = pl.BlockSpec(memory_space=pltpu.VMEM)
    hbm = pl.BlockSpec(memory_space=pl.ANY)
    dma = pltpu.SemaphoreType.DMA
    both, prob = pl.pallas_call(
        functools.partial(moe_kernel, parts, experts, cap),
        out_shape=(
            jax.ShapeDtypeStruct((2, tokens, cols), bf16),
            jax.ShapeDtypeStruct((2, tokens), f32),
        ),
        in_specs=[vmem, vmem, vmem, vmem, hbm, hbm],
        out_specs=(vmem, vmem),
        scratch_shapes=[
            pltpu.VMEM((hidden, width), bf16),
            pltpu.VMEM((hidden, width), bf16),
            pltpu.VMEM((parts, 2, tokens, cols), bf16),
            pltpu.VMEM((tokens, rows), bf16),
            pltpu.VMEM((tokens, rows), bf16),
            pltpu.VMEM((rows, tokens), bf16),
            pltpu.VMEM((rows, 1), f32),
            pltpu.VMEM((parts, experts, 2 * cap, cols), bf16),
            pltpu.VMEM((parts, experts, 2 * cap, cols), bf16),
            pltpu.VMEM((rows, hidden), f32),
            pltpu.VMEM((rows, hidden), f32),
            pltpu.VMEM((rows, hidden), bf16),
            pltpu.VMEM((rows, hidden), bf16),
            pltpu.VMEM((parts, experts, 2 * cap, cols), bf16),
            pltpu.VMEM((parts, experts, 2 * cap, cols), bf16),
            pltpu.VMEM((parts, 2, tokens, cols), bf16),
            pltpu.VMEM((parts, 2, tokens, cols), bf16),
            pltpu.VMEM((2, tokens, cols), f32),
            pltpu.VMEM((tokens, LANES), f32),
            pltpu.VMEM((8, tokens), f32),
            pltpu.VMEM((parts, 8, tokens), f32),
            dma((2,)), dma, dma((parts,)), dma((parts,)), dma, dma((parts,)),
            dma((parts,)), dma, dma((parts,)), dma, dma, dma, dma,
        ],
        compiler_params=pltpu.CompilerParams(
            collective_id=0, has_side_effects=True, vmem_limit_bytes=56 * 1024 * 1024
        ),
    )(inputs, out_grad, gate_probs.T, expert_ids.T, jnp.swapaxes(gate_proj, 1, 2), down_proj)
    layer_out, in_grad, prob_grad = pl.pallas_call(
        split_kernel,
        out_shape=(
            jax.ShapeDtypeStruct((tokens, cols), bf16),
            jax.ShapeDtypeStruct((tokens, cols), bf16),
            jax.ShapeDtypeStruct((2, tokens), f32),
        ),
        in_specs=[vmem, vmem],
        out_specs=(vmem, vmem, vmem),
    )(both, prob)
    return layer_out, in_grad, prob_grad.T


def solution(mesh):
    placed = (
        P("expert", "dp"),
        P("expert", "dp"),
        P("expert", None),
        P("expert", None),
        P("expert", None, "dp"),
        P("expert", "dp", None),
    )
    return jax.shard_map(
        per_device,
        mesh=mesh,
        in_specs=placed,
        out_specs=(P("expert", "dp"), P("expert", "dp"), P("expert", None)),
        check_vma=False,
    )
```

```python
import functools

import jax
import jax.numpy as jnp
from jax import lax
from jax.experimental import pallas as pl
from jax.experimental.pallas import tpu as pltpu
from jax.sharding import PartitionSpec as P

MESH = pl.DeviceIdType.MESH
LANES = 128


def flip(a, b, size):
    out, bit = 0, 1
    while bit < size:
        out = out + ((a // bit + b // bit) % 2) * bit
        bit *= 2
    return out


def nt_dot(left, right):
    return lax.dot_general(
        left, right, (((1,), (1,)), ((), ())), preferred_element_type=jnp.float32
    )


def nn_dot(left, right):
    return jnp.dot(left, right, preferred_element_type=jnp.float32)


def moe_kernel(
    parts, experts, cap,
    x_ref, dy_ref, p_ref, id_ref, wg_hbm, wd_hbm,
    both_ref, pg_ref,
    wg, wd, home, pick0, pick1, spread, weight,
    send, recv, pre, back, hid, gterm, rsend, rrecv,
    part, gathered, own, pacc, psend, precv, fsum, fsend,
    w_sem, ag_send, ag_recv, loc_sem, a_send, a_recv, rloc_sem, r_send, r_recv,
    s_send, s_recv, p_send, p_recv, f_send, f_recv, g_send, g_recv, h_send, h_recv,
    k_send,
):
    z = lax.axis_index("dp")
    me = lax.axis_index("expert")
    far = flip(me, experts - 2, experts)
    tokens, cols = x_ref.shape
    rows = experts * cap
    bf16, f32 = jnp.bfloat16, jnp.float32

    load_g = pltpu.make_async_copy(wg_hbm.at[0], wg, w_sem.at[0])
    load_d = pltpu.make_async_copy(wd_hbm.at[0], wd, w_sem.at[1])
    load_g.start()
    load_d.start()

    barrier = pltpu.get_barrier_semaphore()

    @pl.loop(1, parts)
    def _(i):
        pl.semaphore_signal(
            barrier, inc=1, device_id={"dp": flip(z, i, parts)}, device_id_type=MESH
        )

    @pl.loop(1, experts)
    def _(j):
        pl.semaphore_signal(
            barrier, inc=1, device_id={"expert": flip(me, j, experts)}, device_id_type=MESH
        )

    across = lax.broadcasted_iota(jnp.int32, (tokens, tokens), 1)
    down = lax.broadcasted_iota(jnp.int32, (tokens, tokens), 0)

    def column(row):
        return jnp.sum(jnp.where(across == down, row, 0), axis=1, keepdims=True)

    id0, id1 = column(id_ref[0:1, :]), column(id_ref[1:2, :])
    p0, p1 = column(p_ref[0:1, :]), column(p_ref[1:2, :])
    lane = lax.broadcasted_iota(jnp.int32, (tokens, LANES), 1)
    hot0 = (lane == id0).astype(f32)
    hot1 = (lane == id1).astype(f32)
    earlier = (across < down).astype(f32)
    count = nn_dot(earlier.astype(bf16), (hot0 + hot1).astype(bf16))
    pos0 = jnp.sum(count * hot0, axis=1, keepdims=True)
    pos1 = jnp.sum(count * hot1, axis=1, keepdims=True)
    slot = lax.broadcasted_iota(jnp.int32, (tokens, rows), 1)
    t0 = (slot == id0 * cap + pos0.astype(jnp.int32)).astype(f32)
    t1 = (slot == id1 * cap + pos1.astype(jnp.int32)).astype(f32)
    pick0[...] = t0.astype(bf16)
    pick1[...] = t1.astype(bf16)
    spread[...] = jnp.transpose(t0 + t1).astype(bf16)
    weight[...] = jnp.sum(jnp.transpose(t0 * p0 + t1 * p1), axis=1, keepdims=True)

    home[z, 0] = x_ref[...]
    home[z, 1] = dy_ref[...]
    pre[...] = jnp.zeros_like(pre)
    back[...] = jnp.zeros_like(back)
    pacc[...] = jnp.zeros_like(pacc)

    @pl.loop(1, parts)
    def _(i):
        rrecv[flip(z, i, parts), far] = jnp.zeros((2 * cap, cols), bf16)

    with jax.named_scope("entry"):
        pl.semaphore_wait(barrier, parts - 1 + experts - 1)

    def to_home(i):
        peer = flip(z, i, parts)
        return pltpu.make_async_remote_copy(
            src_ref=home.at[z], dst_ref=home.at[z],
            send_sem=ag_send, recv_sem=ag_recv.at[z],
            device_id={"dp": peer}, device_id_type=MESH,
        )

    @pl.loop(1, parts)
    def _(i):
        to_home(i).start()

    def exchange(source, target, chunk, send_sem, recv_sem, local_sem):
        def put(j):
            peer = flip(me, j, experts)
            pltpu.make_async_remote_copy(
                src_ref=source.at[chunk, peer], dst_ref=target.at[chunk, me],
                send_sem=send_sem, recv_sem=recv_sem.at[chunk],
                device_id={"expert": peer}, device_id_type=MESH,
            ).start()

        put(experts - 1)

        @pl.loop(3, experts)
        def _(j):
            put(experts - j)

        pltpu.make_async_copy(
            source.at[chunk, me], target.at[chunk, me], local_sem.at[chunk]
        ).start()

    def exchanged(source, target, chunk, blocks, recv_sem, local_sem):
        pltpu.make_async_copy(
            source.at[chunk, me], target.at[chunk, me], local_sem.at[chunk]
        ).wait()
        several = target.at[chunk, pl.ds(0, blocks)]
        pltpu.make_async_copy(several, several, recv_sem.at[chunk]).wait()

    def slot_rows(chunk):
        xs = nn_dot(spread[...], home[chunk, 0]).astype(bf16)
        gs = (weight[...] * nn_dot(spread[...], home[chunk, 1])).astype(bf16)
        send[chunk, :, 0:cap] = xs.reshape(experts, cap, cols)
        send[chunk, :, cap:] = gs.reshape(experts, cap, cols)

    slot_rows(z)
    pltpu.make_async_remote_copy(
        src_ref=send.at[z, far], dst_ref=recv.at[z, me],
        send_sem=f_send, recv_sem=f_recv,
        device_id={"expert": far}, device_id_type=MESH,
    ).start()
    exchange(send, recv, z, a_send, a_recv, loc_sem)

    def dispatch(i):
        chunk = flip(z, i, parts)
        pltpu.make_async_copy(home.at[chunk], home.at[chunk], ag_recv.at[chunk]).wait()
        slot_rows(chunk)
        exchange(send, recv, chunk, a_send, a_recv, loc_sem)

    @pl.loop(1, parts - 0)
    def _(i):
        dispatch(i)

    block = recv.at[z, far]
    pltpu.make_async_copy(block, block, f_recv).wait()

    @pl.loop(1, parts)
    def _(i):
        pltpu.make_async_remote_copy(
            src_ref=recv.at[z, far], dst_ref=recv.at[z, far],
            send_sem=g_send, recv_sem=g_recv.at[z],
            device_id={"dp": flip(z, i, parts)}, device_id_type=MESH,
        ).start()

    @pl.loop(parts - 0, parts)
    def _(i):
        dispatch(i)

    load_g.wait()
    load_d.wait()

    def contract(chunk):
        start = pl.multiple_of(chunk * cols, cols)
        exchanged(send, recv, chunk, experts - 2, a_recv, loc_sem)
        xr = recv[chunk, :, 0:cap].reshape(rows, cols)
        gr = recv[chunk, :, cap:].reshape(rows, cols)
        pre[...] += nt_dot(xr, wg[:, pl.ds(start, cols)])
        back[...] += nt_dot(gr, wd[:, pl.ds(start, cols)])

    contract(z)

    @pl.loop(1, parts)
    def _(i):
        chunk = flip(z, i, parts)
        relayed = recv.at[chunk, far]
        pltpu.make_async_copy(relayed, relayed, g_recv.at[chunk]).wait()
        contract(chunk)

    with jax.named_scope("activation"):
        v = pre[...]
        sig = jax.nn.sigmoid(v)
        hid[...] = (v * sig).astype(bf16)
        gterm[...] = (back[...] * sig * (1.0 + v * (1.0 - sig))).astype(bf16)

    def produce(chunk):
        start = pl.multiple_of(chunk * cols, cols)
        out = nn_dot(hid[...], wd[:, pl.ds(start, cols)]).astype(bf16)
        grad = nn_dot(gterm[...], wg[:, pl.ds(start, cols)]).astype(bf16)
        rsend[chunk, :, 0:cap] = out.reshape(experts, cap, cols)
        rsend[chunk, :, cap:] = grad.reshape(experts, cap, cols)

    @pl.loop(1, parts)
    def _(i):
        chunk = flip(z, parts - i, parts)
        produce(chunk)
        pltpu.make_async_remote_copy(
            src_ref=rsend.at[chunk, far], dst_ref=fsum.at[z],
            send_sem=h_send, recv_sem=h_recv,
            device_id={"dp": chunk}, device_id_type=MESH,
        ).start()
        exchange(rsend, rrecv, chunk, r_send, r_recv, rloc_sem)

    produce(z)
    exchange(rsend, rrecv, z, r_send, r_recv, rloc_sem)
    sums = fsum.at[pl.ds(0, parts - 1)]
    pltpu.make_async_copy(sums, sums, h_recv).wait()
    fsend[...] = lax.fori_loop(
        1, parts, lambda i, total: total + fsum[flip(z, i, parts)].astype(f32),
        rsend[z, far].astype(f32),
    ).astype(bf16)
    pltpu.make_async_remote_copy(
        src_ref=fsend, dst_ref=rrecv.at[z, me],
        send_sem=k_send, recv_sem=r_recv.at[z],
        device_id={"expert": far}, device_id_type=MESH,
    ).start()

    def combine(chunk, blocks):
        exchanged(rsend, rrecv, chunk, blocks, r_recv, rloc_sem)
        out = rrecv[chunk, :, 0:cap].reshape(rows, cols)
        grad = rrecv[chunk, :, cap:].reshape(rows, cols)
        out0, out1 = nn_dot(pick0[...], out), nn_dot(pick1[...], out)
        dy = home[chunk, 1].astype(f32)
        s0 = jnp.sum(dy * out0, axis=1, keepdims=True)
        s1 = jnp.sum(dy * out1, axis=1, keepdims=True)
        pacc[...] += jnp.where(lane == 0, s0, 0.0) + jnp.where(lane == 1, s1, 0.0)
        layer = p0 * out0 + p1 * out1
        return layer, nn_dot(pick0[...] + pick1[...], grad)

    def to_owner(chunk):
        return pltpu.make_async_remote_copy(
            src_ref=part.at[chunk], dst_ref=gathered.at[z],
            send_sem=s_send, recv_sem=s_recv,
            device_id={"dp": chunk}, device_id_type=MESH,
        )

    @pl.loop(1, parts)
    def _(i):
        chunk = flip(z, parts - i, parts)
        layer, grad = combine(chunk, experts - 2)
        part[chunk, 0] = layer.astype(bf16)
        part[chunk, 1] = grad.astype(bf16)
        to_owner(chunk).start()

    layer, grad = combine(z, experts - 1)
    own[0] = layer
    own[1] = grad
    psend[...] = jnp.transpose(pacc[...])[0:8]

    @pl.loop(1, parts)
    def _(i):
        pltpu.make_async_remote_copy(
            src_ref=psend, dst_ref=precv.at[z],
            send_sem=p_send, recv_sem=p_recv,
            device_id={"dp": flip(z, i, parts)}, device_id_type=MESH,
        ).start()

    others = gathered.at[pl.ds(0, parts - 1)]
    with jax.named_scope("sums_wait"):
        pltpu.make_async_copy(others, others, s_recv).wait()

    @pl.loop(1, parts)
    def _(i):
        other = flip(z, i, parts)
        own[...] += gathered[other].astype(f32)

    both_ref[...] = own[...].astype(bf16)

    rest = precv.at[pl.ds(0, parts - 1)]
    with jax.named_scope("prob_wait"):
        pltpu.make_async_copy(rest, rest, p_recv).wait()
    pg_ref[...] = psend[0:2]

    @pl.loop(1, parts)
    def _(i):
        pg_ref[...] += precv[flip(z, i, parts), 0:2]

    sent = home.at[pl.ds(0, parts - 1)]
    pltpu.make_async_copy(sent, sent, ag_send).wait()
    pltpu.make_async_copy(others, others, s_send).wait()
    pltpu.make_async_copy(rest, rest, p_send).wait()
    several = send.at[0, pl.ds(0, experts - 2)]

    @pl.loop(0, parts)
    def _(i):
        pltpu.make_async_copy(several, several, a_send).wait()
        pltpu.make_async_copy(several, several, r_send).wait()

    pltpu.make_async_copy(fsend, fsend, f_send).wait()
    pltpu.make_async_copy(fsend, fsend, k_send).wait()
    pltpu.make_async_copy(sums, sums, g_send).wait()
    pltpu.make_async_copy(sums, sums, h_send).wait()


def split_kernel(both_ref, prob_ref, lo_ref, ig_ref, pg_ref):
    lo_ref[...] = both_ref[0]
    ig_ref[...] = both_ref[1]
    pg_ref[...] = prob_ref[...]


def per_device(inputs, out_grad, gate_probs, expert_ids, gate_proj, down_proj):
    parts = lax.axis_size("dp")
    experts = lax.axis_size("expert")
    tokens, cols = inputs.shape
    cap = -(-(3 * tokens // experts) // 16) * 16
    rows = experts * cap
    _, width, hidden = gate_proj.shape
    bf16, f32 = jnp.bfloat16, jnp.float32
    vmem = pl.BlockSpec(memory_space=pltpu.VMEM)
    hbm = pl.BlockSpec(memory_space=pl.ANY)
    dma = pltpu.SemaphoreType.DMA
    both, prob = pl.pallas_call(
        functools.partial(moe_kernel, parts, experts, cap),
        out_shape=(
            jax.ShapeDtypeStruct((2, tokens, cols), bf16),
            jax.ShapeDtypeStruct((2, tokens), f32),
        ),
        in_specs=[vmem, vmem, vmem, vmem, hbm, hbm],
        out_specs=(vmem, vmem),
        scratch_shapes=[
            pltpu.VMEM((hidden, width), bf16),
            pltpu.VMEM((hidden, width), bf16),
            pltpu.VMEM((parts, 2, tokens, cols), bf16),
            pltpu.VMEM((tokens, rows), bf16),
            pltpu.VMEM((tokens, rows), bf16),
            pltpu.VMEM((rows, tokens), bf16),
            pltpu.VMEM((rows, 1), f32),
            pltpu.VMEM((parts, experts, 2 * cap, cols), bf16),
            pltpu.VMEM((parts, experts, 2 * cap, cols), bf16),
            pltpu.VMEM((rows, hidden), f32),
            pltpu.VMEM((rows, hidden), f32),
            pltpu.VMEM((rows, hidden), bf16),
            pltpu.VMEM((rows, hidden), bf16),
            pltpu.VMEM((parts, experts, 2 * cap, cols), bf16),
            pltpu.VMEM((parts, experts, 2 * cap, cols), bf16),
            pltpu.VMEM((parts, 2, tokens, cols), bf16),
            pltpu.VMEM((parts, 2, tokens, cols), bf16),
            pltpu.VMEM((2, tokens, cols), f32),
            pltpu.VMEM((tokens, LANES), f32),
            pltpu.VMEM((8, tokens), f32),
            pltpu.VMEM((parts, 8, tokens), f32),
            pltpu.VMEM((parts, 2 * cap, cols), bf16),
            pltpu.VMEM((2 * cap, cols), bf16),
            dma((2,)), dma, dma((parts,)), dma((parts,)), dma, dma((parts,)),
            dma((parts,)), dma, dma((parts,)), dma, dma, dma, dma,
            dma, dma, dma, dma((parts,)), dma, dma, dma,
        ],
        compiler_params=pltpu.CompilerParams(
            collective_id=0, has_side_effects=True, vmem_limit_bytes=56 * 1024 * 1024
        ),
    )(inputs, out_grad, gate_probs.T, expert_ids.T, jnp.swapaxes(gate_proj, 1, 2), down_proj)
    layer_out, in_grad, prob_grad = pl.pallas_call(
        split_kernel,
        out_shape=(
            jax.ShapeDtypeStruct((tokens, cols), bf16),
            jax.ShapeDtypeStruct((tokens, cols), bf16),
            jax.ShapeDtypeStruct((2, tokens), f32),
        ),
        in_specs=[vmem, vmem],
        out_specs=(vmem, vmem, vmem),
    )(both, prob)
    return layer_out, in_grad, prob_grad.T


def solution(mesh):
    placed = (
        P("expert", "dp"),
        P("expert", "dp"),
        P("expert", None),
        P("expert", None),
        P("expert", None, "dp"),
        P("expert", "dp", None),
    )
    return jax.shard_map(
        per_device,
        mesh=mesh,
        in_specs=placed,
        out_specs=(P("expert", "dp"), P("expert", "dp"), P("expert", None)),
        check_vma=False,
    )
```

```python
import functools

import jax
import jax.numpy as jnp
from jax import lax
from jax.experimental import pallas as pl
from jax.experimental.pallas import tpu as pltpu
from jax.sharding import PartitionSpec as P

MESH = pl.DeviceIdType.MESH
LANES = 128


def flip(a, b, size):
    out, bit = 0, 1
    while bit < size:
        out = out + ((a // bit + b // bit) % 2) * bit
        bit *= 2
    return out


def nt_dot(left, right):
    return lax.dot_general(
        left, right, (((1,), (1,)), ((), ())), preferred_element_type=jnp.float32
    )


def nn_dot(left, right):
    return jnp.dot(left, right, preferred_element_type=jnp.float32)


def moe_kernel(
    parts, experts, cap,
    x_ref, dy_ref, p_ref, id_ref, wg_hbm, wd_hbm,
    both_ref, pg_ref,
    wg, wd, home, pick0, pick1, spread, weight,
    send, recv, pre, back, hid, gterm, rsend, rrecv,
    part, gathered, own, pacc, psend, precv, fsum, fsend,
    w_sem, ag_send, ag_recv, loc_sem, a_send, a_recv, rloc_sem, r_send, r_recv,
    s_send, s_recv, p_send, p_recv, f_send, f_recv, g_send, g_recv, h_send, h_recv,
    k_send,
):
    z = lax.axis_index("dp")
    me = lax.axis_index("expert")
    far = flip(me, experts - 2, experts)
    tokens, cols = x_ref.shape
    rows = experts * cap
    bf16, f32 = jnp.bfloat16, jnp.float32

    load_g = pltpu.make_async_copy(wg_hbm.at[0], wg, w_sem.at[0])
    load_d = pltpu.make_async_copy(wd_hbm.at[0], wd, w_sem.at[1])
    load_g.start()
    load_d.start()

    barrier = pltpu.get_barrier_semaphore()

    @pl.loop(1, parts)
    def _(i):
        pl.semaphore_signal(
            barrier, inc=1, device_id={"dp": flip(z, i, parts)}, device_id_type=MESH
        )

    @pl.loop(1, experts)
    def _(j):
        pl.semaphore_signal(
            barrier, inc=1, device_id={"expert": flip(me, j, experts)}, device_id_type=MESH
        )

    across = lax.broadcasted_iota(jnp.int32, (tokens, tokens), 1)
    down = lax.broadcasted_iota(jnp.int32, (tokens, tokens), 0)

    def column(row):
        return jnp.sum(jnp.where(across == down, row, 0), axis=1, keepdims=True)

    id0, id1 = column(id_ref[0:1, :]), column(id_ref[1:2, :])
    p0, p1 = column(p_ref[0:1, :]), column(p_ref[1:2, :])
    lane = lax.broadcasted_iota(jnp.int32, (tokens, LANES), 1)
    hot0 = (lane == id0).astype(f32)
    hot1 = (lane == id1).astype(f32)
    earlier = (across < down).astype(f32)
    count = nn_dot(earlier.astype(bf16), (hot0 + hot1).astype(bf16))
    pos0 = jnp.sum(count * hot0, axis=1, keepdims=True)
    pos1 = jnp.sum(count * hot1, axis=1, keepdims=True)
    slot = lax.broadcasted_iota(jnp.int32, (tokens, rows), 1)
    t0 = (slot == id0 * cap + pos0.astype(jnp.int32)).astype(f32)
    t1 = (slot == id1 * cap + pos1.astype(jnp.int32)).astype(f32)
    pick0[...] = t0.astype(bf16)
    pick1[...] = t1.astype(bf16)
    spread[...] = jnp.transpose(t0 + t1).astype(bf16)
    weight[...] = jnp.sum(jnp.transpose(t0 * p0 + t1 * p1), axis=1, keepdims=True)

    home[z, 0] = x_ref[...]
    home[z, 1] = dy_ref[...]
    pre[...] = jnp.zeros_like(pre)
    back[...] = jnp.zeros_like(back)
    pacc[...] = jnp.zeros_like(pacc)

    @pl.loop(1, parts)
    def _(i):
        rrecv[flip(z, i, parts), far] = jnp.zeros((2 * cap, cols), bf16)

    with jax.named_scope("entry"):
        pl.semaphore_wait(barrier, parts - 1 + experts - 1)

    rightward, leftward = z + 1 < parts, z > 0

    def pass_on(shard, neighbour):
        return pltpu.make_async_remote_copy(
            src_ref=home.at[shard], dst_ref=home.at[shard],
            send_sem=ag_send, recv_sem=ag_recv.at[shard],
            device_id={"dp": neighbour}, device_id_type=MESH,
        )

    @pl.when(rightward)
    def _():
        pass_on(z, z + 1).start()

    @pl.when(leftward)
    def _():
        pass_on(z, z - 1).start()

    def exchange(source, target, chunk, send_sem, recv_sem, local_sem):
        def put(j):
            peer = flip(me, j, experts)
            pltpu.make_async_remote_copy(
                src_ref=source.at[chunk, peer], dst_ref=target.at[chunk, me],
                send_sem=send_sem, recv_sem=recv_sem.at[chunk],
                device_id={"expert": peer}, device_id_type=MESH,
            ).start()

        put(experts - 1)

        @pl.loop(3, experts)
        def _(j):
            put(experts - j)

        pltpu.make_async_copy(
            source.at[chunk, me], target.at[chunk, me], local_sem.at[chunk]
        ).start()

    def exchanged(source, target, chunk, blocks, recv_sem, local_sem):
        pltpu.make_async_copy(
            source.at[chunk, me], target.at[chunk, me], local_sem.at[chunk]
        ).wait()
        several = target.at[chunk, pl.ds(0, blocks)]
        pltpu.make_async_copy(several, several, recv_sem.at[chunk]).wait()

    def slot_rows(chunk):
        xs = nn_dot(spread[...], home[chunk, 0]).astype(bf16)
        gs = (weight[...] * nn_dot(spread[...], home[chunk, 1])).astype(bf16)
        send[chunk, :, 0:cap] = xs.reshape(experts, cap, cols)
        send[chunk, :, cap:] = gs.reshape(experts, cap, cols)

    slot_rows(z)
    pltpu.make_async_remote_copy(
        src_ref=send.at[z, far], dst_ref=recv.at[z, me],
        send_sem=f_send, recv_sem=f_recv,
        device_id={"expert": far}, device_id_type=MESH,
    ).start()
    exchange(send, recv, z, a_send, a_recv, loc_sem)

    @pl.loop(1, parts)
    def _(i):
        lower, upper = z - i, z + i

        @pl.when(lower >= 0)
        def _():
            shard = home.at[lower]
            pltpu.make_async_copy(shard, shard, ag_recv.at[lower]).wait()

            @pl.when(rightward)
            def _():
                pass_on(lower, z + 1).start()

        @pl.when(upper < parts)
        def _():
            shard = home.at[upper]
            pltpu.make_async_copy(shard, shard, ag_recv.at[upper]).wait()

            @pl.when(leftward)
            def _():
                pass_on(upper, z - 1).start()

        @pl.when(lower >= 0)
        def _():
            slot_rows(lower)
            exchange(send, recv, lower, a_send, a_recv, loc_sem)

        @pl.when(upper < parts)
        def _():
            slot_rows(upper)
            exchange(send, recv, upper, a_send, a_recv, loc_sem)

    block = recv.at[z, far]
    pltpu.make_async_copy(block, block, f_recv).wait()

    @pl.loop(1, parts)
    def _(i):
        pltpu.make_async_remote_copy(
            src_ref=recv.at[z, far], dst_ref=recv.at[z, far],
            send_sem=g_send, recv_sem=g_recv.at[z],
            device_id={"dp": flip(z, i, parts)}, device_id_type=MESH,
        ).start()

    load_g.wait()
    load_d.wait()

    def contract(chunk):
        start = pl.multiple_of(chunk * cols, cols)
        exchanged(send, recv, chunk, experts - 2, a_recv, loc_sem)
        xr = recv[chunk, :, 0:cap].reshape(rows, cols)
        gr = recv[chunk, :, cap:].reshape(rows, cols)
        pre[...] += nt_dot(xr, wg[:, pl.ds(start, cols)])
        back[...] += nt_dot(gr, wd[:, pl.ds(start, cols)])

    contract(z)

    @pl.loop(1, parts)
    def _(i):
        chunk = flip(z, i, parts)
        relayed = recv.at[chunk, far]
        pltpu.make_async_copy(relayed, relayed, g_recv.at[chunk]).wait()
        contract(chunk)

    with jax.named_scope("activation"):
        v = pre[...]
        sig = jax.nn.sigmoid(v)
        hid[...] = (v * sig).astype(bf16)
        gterm[...] = (back[...] * sig * (1.0 + v * (1.0 - sig))).astype(bf16)

    def produce(chunk):
        start = pl.multiple_of(chunk * cols, cols)
        out = nn_dot(hid[...], wd[:, pl.ds(start, cols)]).astype(bf16)
        grad = nn_dot(gterm[...], wg[:, pl.ds(start, cols)]).astype(bf16)
        rsend[chunk, :, 0:cap] = out.reshape(experts, cap, cols)
        rsend[chunk, :, cap:] = grad.reshape(experts, cap, cols)

    @pl.loop(1, parts)
    def _(i):
        chunk = flip(z, parts - i, parts)
        produce(chunk)
        pltpu.make_async_remote_copy(
            src_ref=rsend.at[chunk, far], dst_ref=fsum.at[z],
            send_sem=h_send, recv_sem=h_recv,
            device_id={"dp": chunk}, device_id_type=MESH,
        ).start()
        exchange(rsend, rrecv, chunk, r_send, r_recv, rloc_sem)

    produce(z)
    exchange(rsend, rrecv, z, r_send, r_recv, rloc_sem)
    sums = fsum.at[pl.ds(0, parts - 1)]
    pltpu.make_async_copy(sums, sums, h_recv).wait()
    fsend[...] = lax.fori_loop(
        1, parts, lambda i, total: total + fsum[flip(z, i, parts)].astype(f32),
        rsend[z, far].astype(f32),
    ).astype(bf16)
    pltpu.make_async_remote_copy(
        src_ref=fsend, dst_ref=rrecv.at[z, me],
        send_sem=k_send, recv_sem=r_recv.at[z],
        device_id={"expert": far}, device_id_type=MESH,
    ).start()

    def combine(chunk, blocks):
        exchanged(rsend, rrecv, chunk, blocks, r_recv, rloc_sem)
        out = rrecv[chunk, :, 0:cap].reshape(rows, cols)
        grad = rrecv[chunk, :, cap:].reshape(rows, cols)
        out0, out1 = nn_dot(pick0[...], out), nn_dot(pick1[...], out)
        dy = home[chunk, 1].astype(f32)
        s0 = jnp.sum(dy * out0, axis=1, keepdims=True)
        s1 = jnp.sum(dy * out1, axis=1, keepdims=True)
        pacc[...] += jnp.where(lane == 0, s0, 0.0) + jnp.where(lane == 1, s1, 0.0)
        layer = p0 * out0 + p1 * out1
        return layer, nn_dot(pick0[...] + pick1[...], grad)

    def to_owner(chunk):
        return pltpu.make_async_remote_copy(
            src_ref=part.at[chunk], dst_ref=gathered.at[z],
            send_sem=s_send, recv_sem=s_recv,
            device_id={"dp": chunk}, device_id_type=MESH,
        )

    @pl.loop(1, parts)
    def _(i):
        chunk = flip(z, parts - i, parts)
        layer, grad = combine(chunk, experts - 2)
        part[chunk, 0] = layer.astype(bf16)
        part[chunk, 1] = grad.astype(bf16)
        to_owner(chunk).start()

    layer, grad = combine(z, experts - 1)
    own[0] = layer
    own[1] = grad
    psend[...] = jnp.transpose(pacc[...])[0:8]

    @pl.loop(1, parts)
    def _(i):
        pltpu.make_async_remote_copy(
            src_ref=psend, dst_ref=precv.at[z],
            send_sem=p_send, recv_sem=p_recv,
            device_id={"dp": flip(z, i, parts)}, device_id_type=MESH,
        ).start()

    others = gathered.at[pl.ds(0, parts - 1)]
    with jax.named_scope("sums_wait"):
        pltpu.make_async_copy(others, others, s_recv).wait()

    @pl.loop(1, parts)
    def _(i):
        other = flip(z, i, parts)
        own[...] += gathered[other].astype(f32)

    both_ref[...] = own[...].astype(bf16)

    rest = precv.at[pl.ds(0, parts - 1)]
    with jax.named_scope("prob_wait"):
        pltpu.make_async_copy(rest, rest, p_recv).wait()
    pg_ref[...] = psend[0:2]

    @pl.loop(1, parts)
    def _(i):
        pg_ref[...] += precv[flip(z, i, parts), 0:2]

    passed = home.at[z]

    @pl.when(rightward)
    def _():
        @pl.loop(0, z + 1)
        def _(i):
            pltpu.make_async_copy(passed, passed, ag_send).wait()

    @pl.when(leftward)
    def _():
        @pl.loop(0, parts - z)
        def _(i):
            pltpu.make_async_copy(passed, passed, ag_send).wait()

    pltpu.make_async_copy(others, others, s_send).wait()
    pltpu.make_async_copy(rest, rest, p_send).wait()
    several = send.at[0, pl.ds(0, experts - 2)]

    @pl.loop(0, parts)
    def _(i):
        pltpu.make_async_copy(several, several, a_send).wait()
        pltpu.make_async_copy(several, several, r_send).wait()

    pltpu.make_async_copy(fsend, fsend, f_send).wait()
    pltpu.make_async_copy(fsend, fsend, k_send).wait()
    pltpu.make_async_copy(sums, sums, g_send).wait()
    pltpu.make_async_copy(sums, sums, h_send).wait()


def split_kernel(both_ref, prob_ref, lo_ref, ig_ref, pg_ref):
    lo_ref[...] = both_ref[0]
    ig_ref[...] = both_ref[1]
    pg_ref[...] = prob_ref[...]


def per_device(inputs, out_grad, gate_probs, expert_ids, gate_proj, down_proj):
    parts = lax.axis_size("dp")
    experts = lax.axis_size("expert")
    tokens, cols = inputs.shape
    cap = -(-(3 * tokens // experts) // 16) * 16
    rows = experts * cap
    _, width, hidden = gate_proj.shape
    bf16, f32 = jnp.bfloat16, jnp.float32
    vmem = pl.BlockSpec(memory_space=pltpu.VMEM)
    hbm = pl.BlockSpec(memory_space=pl.ANY)
    dma = pltpu.SemaphoreType.DMA
    both, prob = pl.pallas_call(
        functools.partial(moe_kernel, parts, experts, cap),
        out_shape=(
            jax.ShapeDtypeStruct((2, tokens, cols), bf16),
            jax.ShapeDtypeStruct((2, tokens), f32),
        ),
        in_specs=[vmem, vmem, vmem, vmem, hbm, hbm],
        out_specs=(vmem, vmem),
        scratch_shapes=[
            pltpu.VMEM((hidden, width), bf16),
            pltpu.VMEM((hidden, width), bf16),
            pltpu.VMEM((parts, 2, tokens, cols), bf16),
            pltpu.VMEM((tokens, rows), bf16),
            pltpu.VMEM((tokens, rows), bf16),
            pltpu.VMEM((rows, tokens), bf16),
            pltpu.VMEM((rows, 1), f32),
            pltpu.VMEM((parts, experts, 2 * cap, cols), bf16),
            pltpu.VMEM((parts, experts, 2 * cap, cols), bf16),
            pltpu.VMEM((rows, hidden), f32),
            pltpu.VMEM((rows, hidden), f32),
            pltpu.VMEM((rows, hidden), bf16),
            pltpu.VMEM((rows, hidden), bf16),
            pltpu.VMEM((parts, experts, 2 * cap, cols), bf16),
            pltpu.VMEM((parts, experts, 2 * cap, cols), bf16),
            pltpu.VMEM((parts, 2, tokens, cols), bf16),
            pltpu.VMEM((parts, 2, tokens, cols), bf16),
            pltpu.VMEM((2, tokens, cols), f32),
            pltpu.VMEM((tokens, LANES), f32),
            pltpu.VMEM((8, tokens), f32),
            pltpu.VMEM((parts, 8, tokens), f32),
            pltpu.VMEM((parts, 2 * cap, cols), bf16),
            pltpu.VMEM((2 * cap, cols), bf16),
            dma((2,)), dma, dma((parts,)), dma((parts,)), dma, dma((parts,)),
            dma((parts,)), dma, dma((parts,)), dma, dma, dma, dma,
            dma, dma, dma, dma((parts,)), dma, dma, dma,
        ],
        compiler_params=pltpu.CompilerParams(
            collective_id=0, has_side_effects=True, vmem_limit_bytes=56 * 1024 * 1024
        ),
    )(inputs, out_grad, gate_probs.T, expert_ids.T, jnp.swapaxes(gate_proj, 1, 2), down_proj)
    layer_out, in_grad, prob_grad = pl.pallas_call(
        split_kernel,
        out_shape=(
            jax.ShapeDtypeStruct((tokens, cols), bf16),
            jax.ShapeDtypeStruct((tokens, cols), bf16),
            jax.ShapeDtypeStruct((2, tokens), f32),
        ),
        in_specs=[vmem, vmem],
        out_specs=(vmem, vmem, vmem),
    )(both, prob)
    return layer_out, in_grad, prob_grad.T


def solution(mesh):
    placed = (
        P("expert", "dp"),
        P("expert", "dp"),
        P("expert", None),
        P("expert", None),
        P("expert", None, "dp"),
        P("expert", "dp", None),
    )
    return jax.shard_map(
        per_device,
        mesh=mesh,
        in_specs=placed,
        out_specs=(P("expert", "dp"), P("expert", "dp"), P("expert", None)),
        check_vma=False,
    )
```

```python
import functools

import jax
import jax.numpy as jnp
from jax import lax
from jax.experimental import pallas as pl
from jax.experimental.pallas import tpu as pltpu
from jax.sharding import PartitionSpec as P

MESH = pl.DeviceIdType.MESH
LANES = 128


def flip(a, b, size):
    out, bit = 0, 1
    while bit < size:
        out = out + ((a // bit + b // bit) % 2) * bit
        bit *= 2
    return out


def nt_dot(left, right):
    return lax.dot_general(
        left, right, (((1,), (1,)), ((), ())), preferred_element_type=jnp.float32
    )


def nn_dot(left, right):
    return jnp.dot(left, right, preferred_element_type=jnp.float32)


def moe_kernel(
    parts, experts, cap,
    x_ref, dy_ref, p_ref, id_ref, wg_hbm, wd_hbm,
    both_ref, pg_ref,
    wg, wd, home, pick0, pick1, spread, weight,
    send, recv, pre, back, hid, gterm, rsend, rrecv,
    part, gathered, own, pacc, psend, precv, fsum, fsend,
    w_sem, ag_send, ag_recv, loc_sem, a_send, a_recv, rloc_sem, r_send, r_recv,
    s_send, s_recv, p_send, p_recv, f_send, f_recv, g_send, g_recv, h_send, h_recv,
    k_send,
):
    z = lax.axis_index("dp")
    me = lax.axis_index("expert")
    far = flip(me, experts - 2, experts)
    tokens, cols = x_ref.shape
    rows = experts * cap
    bf16, f32 = jnp.bfloat16, jnp.float32

    load_g = pltpu.make_async_copy(wg_hbm.at[0], wg, w_sem.at[0])
    load_d = pltpu.make_async_copy(wd_hbm.at[0], wd, w_sem.at[1])
    load_g.start()
    load_d.start()

    barrier = pltpu.get_barrier_semaphore()

    @pl.loop(1, parts)
    def _(i):
        pl.semaphore_signal(
            barrier, inc=1, device_id={"dp": flip(z, i, parts)}, device_id_type=MESH
        )

    @pl.loop(1, experts)
    def _(j):
        pl.semaphore_signal(
            barrier, inc=1, device_id={"expert": flip(me, j, experts)}, device_id_type=MESH
        )

    across = lax.broadcasted_iota(jnp.int32, (tokens, tokens), 1)
    down = lax.broadcasted_iota(jnp.int32, (tokens, tokens), 0)

    def column(row):
        return jnp.sum(jnp.where(across == down, row, 0), axis=1, keepdims=True)

    id0, id1 = column(id_ref[0:1, :]), column(id_ref[1:2, :])
    p0, p1 = column(p_ref[0:1, :]), column(p_ref[1:2, :])
    lane = lax.broadcasted_iota(jnp.int32, (tokens, LANES), 1)
    hot0 = (lane == id0).astype(f32)
    hot1 = (lane == id1).astype(f32)
    earlier = (across < down).astype(f32)
    count = nn_dot(earlier.astype(bf16), (hot0 + hot1).astype(bf16))
    pos0 = jnp.sum(count * hot0, axis=1, keepdims=True)
    pos1 = jnp.sum(count * hot1, axis=1, keepdims=True)
    slot = lax.broadcasted_iota(jnp.int32, (tokens, rows), 1)
    t0 = (slot == id0 * cap + pos0.astype(jnp.int32)).astype(f32)
    t1 = (slot == id1 * cap + pos1.astype(jnp.int32)).astype(f32)
    pick0[...] = t0.astype(bf16)
    pick1[...] = t1.astype(bf16)
    spread[...] = jnp.transpose(t0 + t1).astype(bf16)
    weight[...] = jnp.sum(jnp.transpose(t0 * p0 + t1 * p1), axis=1, keepdims=True)

    home[z, 0] = x_ref[...]
    home[z, 1] = dy_ref[...]
    pre[...] = jnp.zeros_like(pre)
    back[...] = jnp.zeros_like(back)
    pacc[...] = jnp.zeros_like(pacc)

    @pl.loop(1, parts)
    def _(i):
        rrecv[flip(z, i, parts), far] = jnp.zeros((2 * cap, cols), bf16)

    with jax.named_scope("entry"):
        pl.semaphore_wait(barrier, parts - 1 + experts - 1)

    rightward, leftward = z + 1 < parts, z > 0

    def pass_on(shard, neighbour):
        return pltpu.make_async_remote_copy(
            src_ref=home.at[shard], dst_ref=home.at[shard],
            send_sem=ag_send, recv_sem=ag_recv.at[shard],
            device_id={"dp": neighbour}, device_id_type=MESH,
        )

    @pl.when(rightward)
    def _():
        pass_on(z, z + 1).start()

    @pl.when(leftward)
    def _():
        pass_on(z, z - 1).start()

    def exchange(source, target, chunk, send_sem, recv_sem, local_sem):
        def put(j):
            peer = flip(me, j, experts)
            pltpu.make_async_remote_copy(
                src_ref=source.at[chunk, peer], dst_ref=target.at[chunk, me],
                send_sem=send_sem, recv_sem=recv_sem.at[chunk],
                device_id={"expert": peer}, device_id_type=MESH,
            ).start()

        put(experts - 1)

        @pl.loop(3, experts)
        def _(j):
            put(experts - j)

        pltpu.make_async_copy(
            source.at[chunk, me], target.at[chunk, me], local_sem.at[chunk]
        ).start()

    def exchanged(source, target, chunk, blocks, recv_sem, local_sem):
        pltpu.make_async_copy(
            source.at[chunk, me], target.at[chunk, me], local_sem.at[chunk]
        ).wait()
        several = target.at[chunk, pl.ds(0, blocks)]
        pltpu.make_async_copy(several, several, recv_sem.at[chunk]).wait()

    def slot_rows(chunk):
        xs = nn_dot(spread[...], home[chunk, 0]).astype(bf16)
        gs = (weight[...] * nn_dot(spread[...], home[chunk, 1])).astype(bf16)
        send[chunk, :, 0:cap] = xs.reshape(experts, cap, cols)
        send[chunk, :, cap:] = gs.reshape(experts, cap, cols)

    slot_rows(z)
    pltpu.make_async_remote_copy(
        src_ref=send.at[z, far], dst_ref=recv.at[z, me],
        send_sem=f_send, recv_sem=f_recv,
        device_id={"expert": far}, device_id_type=MESH,
    ).start()
    exchange(send, recv, z, a_send, a_recv, loc_sem)

    @pl.loop(1, parts)
    def _(i):
        lower, upper = z - i, z + i

        @pl.when(lower >= 0)
        def _():
            shard = home.at[lower]
            pltpu.make_async_copy(shard, shard, ag_recv.at[lower]).wait()

            @pl.when(rightward)
            def _():
                pass_on(lower, z + 1).start()

        @pl.when(upper < parts)
        def _():
            shard = home.at[upper]
            pltpu.make_async_copy(shard, shard, ag_recv.at[upper]).wait()

            @pl.when(leftward)
            def _():
                pass_on(upper, z - 1).start()

        @pl.when(lower >= 0)
        def _():
            slot_rows(lower)
            exchange(send, recv, lower, a_send, a_recv, loc_sem)

        @pl.when(upper < parts)
        def _():
            slot_rows(upper)
            exchange(send, recv, upper, a_send, a_recv, loc_sem)

    block = recv.at[z, far]
    pltpu.make_async_copy(block, block, f_recv).wait()

    @pl.loop(1, parts)
    def _(i):
        pltpu.make_async_remote_copy(
            src_ref=recv.at[z, far], dst_ref=recv.at[z, far],
            send_sem=g_send, recv_sem=g_recv.at[z],
            device_id={"dp": flip(z, i, parts)}, device_id_type=MESH,
        ).start()

    load_g.wait()
    load_d.wait()

    def contract(chunk):
        start = pl.multiple_of(chunk * cols, cols)
        exchanged(send, recv, chunk, experts - 2, a_recv, loc_sem)
        xr = recv[chunk, :, 0:cap].reshape(rows, cols)
        gr = recv[chunk, :, cap:].reshape(rows, cols)
        pre[...] += nt_dot(xr, wg[:, pl.ds(start, cols)])
        back[...] += nt_dot(gr, wd[:, pl.ds(start, cols)])

    contract(z)

    @pl.loop(1, parts)
    def _(i):
        chunk = flip(z, i, parts)
        relayed = recv.at[chunk, far]
        pltpu.make_async_copy(relayed, relayed, g_recv.at[chunk]).wait()
        contract(chunk)

    with jax.named_scope("activation"):
        v = pre[...]
        sig = jax.nn.sigmoid(v)
        hid[...] = (v * sig).astype(bf16)
        gterm[...] = (back[...] * sig * (1.0 + v * (1.0 - sig))).astype(bf16)

    def produce(chunk):
        start = pl.multiple_of(chunk * cols, cols)
        out = nn_dot(hid[...], wd[:, pl.ds(start, cols)]).astype(bf16)
        grad = nn_dot(gterm[...], wg[:, pl.ds(start, cols)]).astype(bf16)
        rsend[chunk, :, 0:cap] = out.reshape(experts, cap, cols)
        rsend[chunk, :, cap:] = grad.reshape(experts, cap, cols)

    def farthest_first(body):
        @pl.loop(1, parts)
        def _(i):
            lower, upper = z - (parts - i), z + (parts - i)

            @pl.when(lower >= 0)
            def _():
                body(lower)

            @pl.when(upper < parts)
            def _():
                body(upper)

    def give_back(chunk):
        produce(chunk)
        pltpu.make_async_remote_copy(
            src_ref=rsend.at[chunk, far], dst_ref=fsum.at[z],
            send_sem=h_send, recv_sem=h_recv,
            device_id={"dp": chunk}, device_id_type=MESH,
        ).start()
        exchange(rsend, rrecv, chunk, r_send, r_recv, rloc_sem)

    farthest_first(give_back)
    produce(z)
    exchange(rsend, rrecv, z, r_send, r_recv, rloc_sem)
    sums = fsum.at[pl.ds(0, parts - 1)]
    pltpu.make_async_copy(sums, sums, h_recv).wait()
    fsend[...] = lax.fori_loop(
        1, parts, lambda i, total: total + fsum[flip(z, i, parts)].astype(f32),
        rsend[z, far].astype(f32),
    ).astype(bf16)
    pltpu.make_async_remote_copy(
        src_ref=fsend, dst_ref=rrecv.at[z, me],
        send_sem=k_send, recv_sem=r_recv.at[z],
        device_id={"expert": far}, device_id_type=MESH,
    ).start()

    def combine(chunk, blocks):
        exchanged(rsend, rrecv, chunk, blocks, r_recv, rloc_sem)
        out = rrecv[chunk, :, 0:cap].reshape(rows, cols)
        grad = rrecv[chunk, :, cap:].reshape(rows, cols)
        out0, out1 = nn_dot(pick0[...], out), nn_dot(pick1[...], out)
        dy = home[chunk, 1].astype(f32)
        s0 = jnp.sum(dy * out0, axis=1, keepdims=True)
        s1 = jnp.sum(dy * out1, axis=1, keepdims=True)
        pacc[...] += jnp.where(lane == 0, s0, 0.0) + jnp.where(lane == 1, s1, 0.0)
        layer = p0 * out0 + p1 * out1
        return layer, nn_dot(pick0[...] + pick1[...], grad)

    def add_from(side, chunk):
        arrived = gathered.at[side, chunk]
        pltpu.make_async_copy(arrived, arrived, s_recv.at[side, chunk]).wait()
        own[...] += gathered[side, chunk].astype(f32)

    def hand_on(side, chunk, neighbour):
        pltpu.make_async_remote_copy(
            src_ref=part.at[chunk], dst_ref=gathered.at[side, chunk],
            send_sem=s_send, recv_sem=s_recv.at[side, chunk],
            device_id={"dp": neighbour}, device_id_type=MESH,
        ).start()

    def sum_on(chunk):
        layer, grad = combine(chunk, experts - 2)
        own[0] = layer
        own[1] = grad

        @pl.when((chunk > z) & leftward)
        def _():
            add_from(0, chunk)

        @pl.when((chunk < z) & rightward)
        def _():
            add_from(1, chunk)

        part[chunk] = own[...].astype(bf16)

        @pl.when(chunk > z)
        def _():
            hand_on(0, chunk, z + 1)

        @pl.when(chunk < z)
        def _():
            hand_on(1, chunk, z - 1)

    farthest_first(sum_on)

    layer, grad = combine(z, experts - 1)
    own[0] = layer
    own[1] = grad
    psend[...] = jnp.transpose(pacc[...])[0:8]

    @pl.loop(1, parts)
    def _(i):
        pltpu.make_async_remote_copy(
            src_ref=psend, dst_ref=precv.at[z],
            send_sem=p_send, recv_sem=p_recv,
            device_id={"dp": flip(z, i, parts)}, device_id_type=MESH,
        ).start()

    @pl.when(leftward)
    def _():
        add_from(0, z)

    @pl.when(rightward)
    def _():
        add_from(1, z)

    both_ref[...] = own[...].astype(bf16)

    rest = precv.at[pl.ds(0, parts - 1)]
    with jax.named_scope("prob_wait"):
        pltpu.make_async_copy(rest, rest, p_recv).wait()
    pg_ref[...] = psend[0:2]

    @pl.loop(1, parts)
    def _(i):
        pg_ref[...] += precv[flip(z, i, parts), 0:2]

    passed = home.at[z]

    @pl.when(rightward)
    def _():
        @pl.loop(0, z + 1)
        def _(i):
            pltpu.make_async_copy(passed, passed, ag_send).wait()

    @pl.when(leftward)
    def _():
        @pl.loop(0, parts - z)
        def _(i):
            pltpu.make_async_copy(passed, passed, ag_send).wait()

    others = part.at[pl.ds(0, parts - 1)]
    pltpu.make_async_copy(others, others, s_send).wait()
    pltpu.make_async_copy(rest, rest, p_send).wait()
    several = send.at[0, pl.ds(0, experts - 2)]

    @pl.loop(0, parts)
    def _(i):
        pltpu.make_async_copy(several, several, a_send).wait()
        pltpu.make_async_copy(several, several, r_send).wait()

    pltpu.make_async_copy(fsend, fsend, f_send).wait()
    pltpu.make_async_copy(fsend, fsend, k_send).wait()
    pltpu.make_async_copy(sums, sums, g_send).wait()
    pltpu.make_async_copy(sums, sums, h_send).wait()


def split_kernel(both_ref, prob_ref, lo_ref, ig_ref, pg_ref):
    lo_ref[...] = both_ref[0]
    ig_ref[...] = both_ref[1]
    pg_ref[...] = prob_ref[...]


def per_device(inputs, out_grad, gate_probs, expert_ids, gate_proj, down_proj):
    parts = lax.axis_size("dp")
    experts = lax.axis_size("expert")
    tokens, cols = inputs.shape
    cap = -(-(3 * tokens // experts) // 16) * 16
    rows = experts * cap
    _, width, hidden = gate_proj.shape
    bf16, f32 = jnp.bfloat16, jnp.float32
    vmem = pl.BlockSpec(memory_space=pltpu.VMEM)
    hbm = pl.BlockSpec(memory_space=pl.ANY)
    dma = pltpu.SemaphoreType.DMA
    both, prob = pl.pallas_call(
        functools.partial(moe_kernel, parts, experts, cap),
        out_shape=(
            jax.ShapeDtypeStruct((2, tokens, cols), bf16),
            jax.ShapeDtypeStruct((2, tokens), f32),
        ),
        in_specs=[vmem, vmem, vmem, vmem, hbm, hbm],
        out_specs=(vmem, vmem),
        scratch_shapes=[
            pltpu.VMEM((hidden, width), bf16),
            pltpu.VMEM((hidden, width), bf16),
            pltpu.VMEM((parts, 2, tokens, cols), bf16),
            pltpu.VMEM((tokens, rows), bf16),
            pltpu.VMEM((tokens, rows), bf16),
            pltpu.VMEM((rows, tokens), bf16),
            pltpu.VMEM((rows, 1), f32),
            pltpu.VMEM((parts, experts, 2 * cap, cols), bf16),
            pltpu.VMEM((parts, experts, 2 * cap, cols), bf16),
            pltpu.VMEM((rows, hidden), f32),
            pltpu.VMEM((rows, hidden), f32),
            pltpu.VMEM((rows, hidden), bf16),
            pltpu.VMEM((rows, hidden), bf16),
            pltpu.VMEM((parts, experts, 2 * cap, cols), bf16),
            pltpu.VMEM((parts, experts, 2 * cap, cols), bf16),
            pltpu.VMEM((parts, 2, tokens, cols), bf16),
            pltpu.VMEM((2, parts, 2, tokens, cols), bf16),
            pltpu.VMEM((2, tokens, cols), f32),
            pltpu.VMEM((tokens, LANES), f32),
            pltpu.VMEM((8, tokens), f32),
            pltpu.VMEM((parts, 8, tokens), f32),
            pltpu.VMEM((parts, 2 * cap, cols), bf16),
            pltpu.VMEM((2 * cap, cols), bf16),
            dma((2,)), dma, dma((parts,)), dma((parts,)), dma, dma((parts,)),
            dma((parts,)), dma, dma((parts,)), dma, dma((2, parts)), dma, dma,
            dma, dma, dma, dma((parts,)), dma, dma, dma,
        ],
        compiler_params=pltpu.CompilerParams(
            collective_id=0, has_side_effects=True, vmem_limit_bytes=56 * 1024 * 1024
        ),
    )(inputs, out_grad, gate_probs.T, expert_ids.T, jnp.swapaxes(gate_proj, 1, 2), down_proj)
    layer_out, in_grad, prob_grad = pl.pallas_call(
        split_kernel,
        out_shape=(
            jax.ShapeDtypeStruct((tokens, cols), bf16),
            jax.ShapeDtypeStruct((tokens, cols), bf16),
            jax.ShapeDtypeStruct((2, tokens), f32),
        ),
        in_specs=[vmem, vmem],
        out_specs=(vmem, vmem, vmem),
    )(both, prob)
    return layer_out, in_grad, prob_grad.T


def solution(mesh):
    placed = (
        P("expert", "dp"),
        P("expert", "dp"),
        P("expert", None),
        P("expert", None),
        P("expert", None, "dp"),
        P("expert", "dp", None),
    )
    return jax.shard_map(
        per_device,
        mesh=mesh,
        in_specs=placed,
        out_specs=(P("expert", "dp"), P("expert", "dp"), P("expert", None)),
        check_vma=False,
    )
```
